256 devices in a mesh: seq: 32 (over z_hi, x, core), head: 8 (over y, z_lo).
Axes of the slice: x: 4, y: 4, z: 8 (z_hi: 4, z_lo: 2; z = z_hi * 2 + z_lo), core: 2. Of those that a mesh axis runs over, the one named last changes fastest.
Arguments:
- queries: bfloat16 [512, 40, 128], P('seq', 'head'), may hold values from -6 to 6
- document_key_rows: bfloat16 [65536, 8, 128], P('seq', 'head'), may hold values from -16 to 16
- document_value_rows: bfloat16 [65536, 8, 128], P('seq', 'head'), may hold values from -6 to 6
- out_gain: float32 [40, 128], P('head'), may hold values from 0.1 to 1.9
- out_weight: bfloat16 [5120, 5120], P('head'), may hold values from -0.078125 to 0.078125
Outputs:
- mixed_out: bfloat16 [512, 5120], P('seq', 'head')
The draws below stay inside these ranges and needn't reach their ends.
All inputs are finite; a program needn't handle non-finite values.
Results may differ from the reference program's by a relative error of at most 0.03.
Values may be sent and summed in bfloat16 or wider, within the bound.
No kernel may reach another device: no remote copies, remote signals or barrier semaphores. Data moves between devices by JAX's collectives and lax.ppermute only.
A program may use at most 64 MiB of HBM per device.

```python
import math
import jax
import jax.numpy as jnp
from jax import lax

D = 5120
QUERY_HEADS = 40
KEY_VALUE_HEADS = 8
HEAD_SIZE = 128
LOCAL_TOKENS = 2048
DOCUMENT_TOKENS = 65536
CANDIDATE_ROWS = 512
N_SEQ = 32


def draw_document_key_rows(key, part):
    key_baseline, sampled_key_rows = jax.random.split(key, 2)
    position = jnp.arange(DOCUMENT_TOKENS, dtype=jnp.float32) / max(DOCUMENT_TOKENS - 1, 1)
    ramp_scale = jnp.sqrt(1.0 + 2.0 * position)[:, None, None]
    per_row_scale = jnp.exp(jax.random.uniform(sampled_key_rows, (DOCUMENT_TOKENS, KEY_VALUE_HEADS, 1), minval=-0.6, maxval=0.6))
    baseline_sample = jax.random.normal(key_baseline, (DOCUMENT_TOKENS, KEY_VALUE_HEADS, HEAD_SIZE))
    return jnp.clip(baseline_sample * ramp_scale * per_row_scale, -16.0, 16.0).astype(jnp.bfloat16)


def steps_of(rng, extent, shards, smallest, largest):
    factor_of = 1.0
    for dim, blocks in shards:
        draws = jax.random.uniform(jax.random.fold_in(jax.random.fold_in(rng, 6), dim), (blocks,), jnp.float32, smallest / len(shards), largest / len(shards))
        factor_of = factor_of * jnp.repeat(jnp.exp(draws), extent[dim] // blocks).reshape((-1,) + (1,) * (len(extent) - 1 - dim))
    return factor_of


def scatter_about(key, extent, spread, most, shards=(), kind=jnp.bfloat16):
    factor_of = steps_of(key, extent, shards, -0.22, 0.18) if shards else 1.0
    entries = jax.random.normal(key, extent, jnp.float32) * spread * factor_of
    return jnp.minimum(jnp.maximum(entries, -most), most).astype(kind)


def setup_inputs(seed: int = 0) -> dict:
    arg_keys = jax.random.split(jax.random.key(seed), 6)
    return {
        "queries": scatter_about(arg_keys[0], (CANDIDATE_ROWS, QUERY_HEADS, HEAD_SIZE), 1.0, 6.0, ((0, 32), (1, 8))),
        "document_key_rows": draw_document_key_rows(jax.random.fold_in(arg_keys[5], 71), 0),
        "document_value_rows": scatter_about(arg_keys[2], (DOCUMENT_TOKENS, KEY_VALUE_HEADS, HEAD_SIZE), 1.0, 6.0, ((0, 32), (1, 8))),
        "out_gain": jnp.clip(1.0 + 0.18 * jax.random.normal(arg_keys[3], (QUERY_HEADS, HEAD_SIZE), jnp.float32), 0.1, 1.9),
        "out_weight": scatter_about(arg_keys[4], (QUERY_HEADS * HEAD_SIZE, D), (QUERY_HEADS * HEAD_SIZE) ** -0.5, 0.078125, ((0, 8),)),
    }


SQRT_TWO = math.sqrt(2.0)

def features(values_in):
    head_dim = values_in.shape[-1]
    widened = values_in.astype(jnp.float32)
    pieces = []
    for shift_now in range(head_dim // 2 + 1):
        factor = 1.0 if shift_now == 0 else SQRT_TWO
        pieces.append(widened * jnp.roll(widened, -shift_now, axis=-1) * factor)
    joined = jnp.concatenate(pieces, axis=-1)
    return joined[..., :head_dim * (head_dim + 1) // 2].astype(jnp.bfloat16)

def reference(queries, document_key_rows, document_value_rows, out_gain, out_weight):
    feature_dim = HEAD_SIZE * (HEAD_SIZE + 1) // 2
    key_per_head = jnp.transpose(document_key_rows, (1, 0, 2)).reshape(KEY_VALUE_HEADS, N_SEQ, LOCAL_TOKENS, HEAD_SIZE)
    value_per_head = jnp.transpose(document_value_rows, (1, 0, 2)).reshape(KEY_VALUE_HEADS, N_SEQ, LOCAL_TOKENS, HEAD_SIZE)

    def block_sum(total, pair):
        key_feats = features(pair[0])
        partial_value = jnp.dot(key_feats.T, pair[1], preferred_element_type=jnp.float32).astype(jnp.bfloat16)
        return (total + partial_value.astype(jnp.float32), None)

    def head_state(pair):
        total, _ = lax.scan(block_sum, jnp.zeros((feature_dim, HEAD_SIZE), jnp.float32), pair)
        return total.astype(jnp.bfloat16)
    states = lax.map(head_state, (key_per_head, value_per_head))
    query_group_width = QUERY_HEADS // KEY_VALUE_HEADS
    query_per_head = jnp.transpose(queries.reshape(CANDIDATE_ROWS, KEY_VALUE_HEADS, query_group_width, HEAD_SIZE), (1, 0, 2, 3))

    def head_read(pair):
        query_feats = features(pair[0]).reshape(CANDIDATE_ROWS * query_group_width, feature_dim)
        read_out = jnp.dot(query_feats, pair[1], preferred_element_type=jnp.float32)
        return read_out.reshape(CANDIDATE_ROWS, query_group_width, HEAD_SIZE)
    reads = lax.map(head_read, (query_per_head, states))
    retained = jnp.transpose(reads, (1, 0, 2, 3)).reshape(CANDIDATE_ROWS, QUERY_HEADS, HEAD_SIZE)
    mean_square = lax.optimization_barrier(jnp.mean(retained * retained, axis=-1, keepdims=True))
    normed = (retained * lax.rsqrt(mean_square + 1e-06) * out_gain).astype(jnp.bfloat16)
    flat = normed.reshape(CANDIDATE_ROWS, QUERY_HEADS * HEAD_SIZE)
    return jnp.dot(flat, out_weight, preferred_element_type=jnp.float32).astype(jnp.bfloat16)
```

```python
import jax
import jax.numpy as jnp
from jax import lax
from jax.experimental import pallas as pl
from jax.experimental.pallas import tpu as pltpu
from jax.sharding import PartitionSpec as P

CONTRACT_LAST = (((1,), (1,)), ((), ()))
KEY_TILE = 256
X_CHIPS, Z_BLOCKS, CORES = 4, 4, 2


def seq_index(z_block, x_chip, core):
    return (z_block * X_CHIPS + x_chip) * CORES + core


def same_core_groups():
    return [
        [seq_index(z, x, core) for z in range(Z_BLOCKS) for x in range(X_CHIPS)]
        for core in range(CORES)
    ]


def read_kernel(q_ref, k0_ref, k1_ref, v0_ref, v1_ref, o_ref):
    rows = q_ref[...]
    total = None
    for k_ref, v_ref in ((k0_ref, v0_ref), (k1_ref, v1_ref)):
        for start in range(0, k_ref.shape[0], KEY_TILE):
            tile = pl.ds(start, KEY_TILE)
            scores = lax.dot_general(
                rows, k_ref[tile, :], CONTRACT_LAST, preferred_element_type=jnp.float32
            )
            weights = (scores * scores).astype(jnp.bfloat16)
            term = jnp.dot(weights, v_ref[tile, :], preferred_element_type=jnp.float32)
            total = term if total is None else total + term
    o_ref[...] = total.astype(o_ref.dtype)


def read_document(rows, keys, values):
    vmem = pl.BlockSpec(memory_space=pltpu.VMEM)
    return pl.pallas_call(
        read_kernel,
        out_shape=jax.ShapeDtypeStruct(rows.shape, jnp.bfloat16),
        in_specs=[vmem] * 5,
        out_specs=vmem,
        compiler_params=pltpu.CompilerParams(vmem_limit_bytes=24 << 20),
        name="read_document",
    )(rows, *keys, *values)


def project_kernel(parts_ref, gain_ref, weight_ref, o_ref):
    retained = jnp.sum(parts_ref[...].astype(jnp.float32), axis=0)
    heads, width = gain_ref.shape
    rows = retained.shape[0] // heads
    pieces = []
    for h in range(heads):
        one = retained[h * rows : (h + 1) * rows, :]
        mean_square = jnp.mean(one * one, axis=-1, keepdims=True)
        normed = one * lax.rsqrt(mean_square + 1e-06) * gain_ref[pl.ds(h, 1), :]
        pieces.append(normed.astype(jnp.bfloat16))
    flat = jnp.concatenate(pieces, axis=1)
    chunk = o_ref.shape[2]
    for g in range(o_ref.shape[0]):
        o_ref[g] = jnp.dot(
            flat, weight_ref[:, g * chunk : (g + 1) * chunk], preferred_element_type=jnp.float32
        ).astype(o_ref.dtype)


def project(parts, gain, weight, groups):
    vmem = pl.BlockSpec(memory_space=pltpu.VMEM)
    rows = parts.shape[1] // gain.shape[0]
    return pl.pallas_call(
        project_kernel,
        out_shape=jax.ShapeDtypeStruct((groups, rows, weight.shape[1] // groups), jnp.bfloat16),
        in_specs=[vmem] * 3,
        out_specs=vmem,
        compiler_params=pltpu.CompilerParams(vmem_limit_bytes=24 << 20),
        name="project",
    )(parts, gain, weight)


def on_device(queries, document_key_rows, document_value_rows, out_gain, out_weight):
    rows, heads, width = queries.shape
    tokens = document_key_rows.shape[0]
    peers = same_core_groups()
    peer_count = len(peers[0])
    head_groups = lax.axis_size("head")
    keys = document_key_rows.reshape(tokens, width)
    values = document_value_rows.reshape(tokens, width)
    other_core = [(i, i ^ 1) for i in range(lax.axis_size("seq"))]
    other_keys = lax.ppermute(keys, "seq", other_core)
    other_values = lax.ppermute(values, "seq", other_core)
    own = jnp.transpose(queries, (1, 0, 2)).reshape(heads * rows, width)
    copies = jnp.broadcast_to(own[None], (peer_count, heads * rows, width))
    gathered = lax.all_to_all(copies, "seq", 0, 0, axis_index_groups=peers, tiled=True)
    partial = read_document(
        gathered.reshape(peer_count * heads * rows, width),
        (keys, other_keys),
        (values, other_values),
    ).reshape(peer_count, heads * rows, width)
    parts = lax.all_to_all(partial, "seq", 0, 0, axis_index_groups=peers, tiled=True)
    projected = project(parts, out_gain, out_weight, head_groups)
    pieces = lax.all_to_all(projected, "head", 0, 0, tiled=True)
    return jnp.sum(pieces.astype(jnp.float32), axis=0).astype(jnp.bfloat16)


def solution(mesh):
    in_specs = (
        P("seq", "head", None),
        P("seq", "head", None),
        P("seq", "head", None),
        P("head", None),
        P("head", None),
    )
    out_specs = P("seq", "head")
    return jax.shard_map(
        on_device, mesh=mesh, in_specs=in_specs, out_specs=out_specs, check_vma=False
    )
```

```python
import jax
import jax.numpy as jnp
from jax import lax
from jax.experimental import pallas as pl
from jax.experimental.pallas import tpu as pltpu
from jax.sharding import PartitionSpec as P

CONTRACT_LAST = (((1,), (1,)), ((), ()))
KEY_TILE = 256
X_CHIPS, Z_BLOCKS, CORES = 4, 4, 2


def seq_index(z_block, x_chip, core):
    return (z_block * X_CHIPS + x_chip) * CORES + core


def same_core_groups():
    return [
        [seq_index(z, x, core) for z in range(Z_BLOCKS) for x in range(X_CHIPS)]
        for core in range(CORES)
    ]


def read_kernel(
    q_ref,
    k_near_ref,
    v_near_ref,
    k_hbm,
    v_hbm,
    weight_hbm,
    gain_hbm,
    o_ref,
    weight_ref,
    gain_ref,
    k_own_ref,
    v_own_ref,
    sems,
):
    copies = [
        pltpu.make_async_copy(src, dst, sems.at[i])
        for i, (src, dst) in enumerate(
            ((k_hbm, k_own_ref), (v_hbm, v_own_ref), (weight_hbm, weight_ref), (gain_hbm, gain_ref))
        )
    ]
    for copy in copies:
        copy.start()
    rows = q_ref[...]
    total = None
    for k_ref, v_ref in ((k_near_ref, v_near_ref), (k_own_ref, v_own_ref)):
        if k_ref is k_own_ref:
            copies[0].wait()
            copies[1].wait()
        for start in range(0, k_ref.shape[0], KEY_TILE):
            tile = pl.ds(start, KEY_TILE)
            scores = lax.dot_general(
                rows, k_ref[tile, :], CONTRACT_LAST, preferred_element_type=jnp.float32
            )
            weights = (scores * scores).astype(jnp.bfloat16)
            term = jnp.dot(weights, v_ref[tile, :], preferred_element_type=jnp.float32)
            total = term if total is None else total + term
    o_ref[...] = total.astype(o_ref.dtype)
    copies[2].wait()
    copies[3].wait()


def read_document(rows, near, own, weight, gain):
    vmem = pl.BlockSpec(memory_space=pltpu.VMEM)
    hbm = pl.BlockSpec(memory_space=pltpu.HBM)
    return pl.pallas_call(
        read_kernel,
        out_shape=(
            jax.ShapeDtypeStruct(rows.shape, jnp.bfloat16),
            jax.ShapeDtypeStruct(weight.shape, weight.dtype),
            jax.ShapeDtypeStruct(gain.shape, gain.dtype),
        ),
        in_specs=[vmem] * 3 + [hbm] * 4,
        out_specs=(vmem, vmem, vmem),
        scratch_shapes=[
            pltpu.VMEM(own[0].shape, own[0].dtype),
            pltpu.VMEM(own[1].shape, own[1].dtype),
            pltpu.SemaphoreType.DMA((4,)),
        ],
        compiler_params=pltpu.CompilerParams(vmem_limit_bytes=32 << 20),
        name="read_document",
    )(
        rows,
        *near,
        *(pltpu.with_memory_space_constraint(a, pltpu.HBM) for a in (*own, weight, gain)),
    )


def project_kernel(parts_ref, gain_ref, weight_ref, o_ref):
    retained = jnp.sum(parts_ref[...].astype(jnp.float32), axis=0)
    heads, width = gain_ref.shape
    rows = retained.shape[0] // heads
    pieces = []
    for h in range(heads):
        one = retained[h * rows : (h + 1) * rows, :]
        mean_square = jnp.mean(one * one, axis=-1, keepdims=True)
        normed = one * lax.rsqrt(mean_square + 1e-06) * gain_ref[pl.ds(h, 1), :]
        pieces.append(normed.astype(jnp.bfloat16))
    flat = jnp.concatenate(pieces, axis=1)
    chunk = o_ref.shape[2]
    for g in range(o_ref.shape[0]):
        o_ref[g] = jnp.dot(
            flat, weight_ref[:, g * chunk : (g + 1) * chunk], preferred_element_type=jnp.float32
        ).astype(o_ref.dtype)


def project(parts, gain, weight, groups):
    vmem = pl.BlockSpec(memory_space=pltpu.VMEM)
    rows = parts.shape[1] // gain.shape[0]
    return pl.pallas_call(
        project_kernel,
        out_shape=jax.ShapeDtypeStruct((groups, rows, weight.shape[1] // groups), jnp.bfloat16),
        in_specs=[vmem] * 3,
        out_specs=vmem,
        compiler_params=pltpu.CompilerParams(vmem_limit_bytes=24 << 20),
        name="project",
    )(parts, gain, weight)


def on_device(queries, document_key_rows, document_value_rows, out_gain, out_weight):
    rows, heads, width = queries.shape
    tokens = document_key_rows.shape[0]
    peers = same_core_groups()
    peer_count = len(peers[0])
    head_groups = lax.axis_size("head")
    keys = document_key_rows.reshape(tokens, width)
    values = document_value_rows.reshape(tokens, width)
    other_core = [(i, i ^ 1) for i in range(lax.axis_size("seq"))]
    other_keys = lax.ppermute(keys, "seq", other_core)
    other_values = lax.ppermute(values, "seq", other_core)
    own = jnp.transpose(queries, (1, 0, 2)).reshape(heads * rows, width)
    copies = jnp.broadcast_to(own[None], (peer_count, heads * rows, width))
    gathered = lax.all_to_all(copies, "seq", 0, 0, axis_index_groups=peers, tiled=True)
    partial, weight, gain = read_document(
        gathered.reshape(peer_count * heads * rows, width),
        (other_keys, other_values),
        (keys, values),
        out_weight,
        out_gain,
    )
    partial = partial.reshape(peer_count, heads * rows, width)
    parts = lax.all_to_all(partial, "seq", 0, 0, axis_index_groups=peers, tiled=True)
    projected = project(parts, gain, weight, head_groups)
    pieces = lax.all_to_all(projected, "head", 0, 0, tiled=True)
    return jnp.sum(pieces.astype(jnp.float32), axis=0).astype(jnp.bfloat16)


def solution(mesh):
    in_specs = (
        P("seq", "head", None),
        P("seq", "head", None),
        P("seq", "head", None),
        P("head", None),
        P("head", None),
    )
    out_specs = P("seq", "head")
    return jax.shard_map(
        on_device, mesh=mesh, in_specs=in_specs, out_specs=out_specs, check_vma=False
    )
```

```python
import functools

import jax
import jax.numpy as jnp
from jax import lax
from jax.experimental import pallas as pl
from jax.experimental.pallas import tpu as pltpu
from jax.sharding import PartitionSpec as P

CONTRACT_LAST = (((1,), (1,)), ((), ()))
KEY_TILE = 256
X_CHIPS, Z_BLOCKS, CORES = 4, 4, 2
ORDER = (2, 3, 1)


def seq_index(z_block, x_chip, core):
    return (z_block * X_CHIPS + x_chip) * CORES + core


def exchange(rows, z_step, x_step, core_step):
    pairs = []
    for z in range(Z_BLOCKS):
        for x in range(X_CHIPS):
            for core in range(CORES):
                to = seq_index(z ^ z_step, x ^ x_step, core ^ core_step)
                pairs.append((seq_index(z, x, core), to))
    return lax.ppermute(rows, "seq", pairs)


VMEM = pl.BlockSpec(memory_space=pltpu.VMEM)
HBM = pl.BlockSpec(memory_space=pltpu.HBM)


def in_hbm(array):
    return pltpu.with_memory_space_constraint(array, pltpu.HBM)


def params(mib):
    return pltpu.CompilerParams(vmem_limit_bytes=mib << 20)


def stage_kernel(*refs):
    count = len(refs) // 2
    copies = []
    for i in range(count):
        source, target = refs[i], refs[count + i]
        if source.shape != target.shape:
            source = source.at[pl.ds(0, target.shape[0]), :]
        copies.append(pltpu.make_async_copy(source, target, refs[-1].at[i]))
    for copy in copies:
        copy.start()
    for copy in copies:
        copy.wait()


def stage(*arrays, row_counts):
    return pl.pallas_call(
        stage_kernel,
        out_shape=tuple(
            jax.ShapeDtypeStruct((count,) + a.shape[1:], a.dtype)
            for a, count in zip(arrays, row_counts)
        ),
        in_specs=[HBM] * len(arrays),
        out_specs=(VMEM,) * len(arrays),
        scratch_shapes=[pltpu.SemaphoreType.DMA((len(arrays),))],
        compiler_params=params(4),
        cost_estimate=pl.CostEstimate(flops=0, bytes_accessed=4 << 20, transcendentals=0),
        name="stage",
    )(*(in_hbm(a) for a in arrays))


def join_kernel(*refs):
    for i, ref in enumerate(refs[:-1]):
        refs[-1][i] = ref[...]


def join(arrays):
    shape = (len(arrays),) + arrays[0].shape
    return pl.pallas_call(
        join_kernel,
        out_shape=jax.ShapeDtypeStruct(shape, arrays[0].dtype),
        in_specs=[VMEM] * len(arrays),
        out_specs=VMEM,
        compiler_params=params(2),
        name="join",
    )(*arrays)


def read_rows(q_ref, pairs, o_ref):
    chunks, count, width = q_ref.shape
    rows = q_ref[...].reshape(chunks * count, width)
    total = None
    for k_ref, v_ref in pairs:
        for start in range(0, k_ref.shape[0], KEY_TILE):
            tile = pl.ds(start, KEY_TILE)
            scores = lax.dot_general(
                rows, k_ref[tile, :], CONTRACT_LAST, preferred_element_type=jnp.float32
            )
            weights = (scores * scores).astype(jnp.bfloat16)
            term = jnp.dot(weights, v_ref[tile, :], preferred_element_type=jnp.float32)
            total = term if total is None else total + term
    o_ref[...] = total.astype(o_ref.dtype).reshape(q_ref.shape)


def read_kernel(q_ref, k0_ref, v0_ref, k1_ref, v1_ref, after_ref, o_ref):
    read_rows(q_ref, ((k0_ref, v0_ref), (k1_ref, v1_ref)), o_ref)


def read(rows, document, after):
    tokens = sum(a.shape[0] for a in document) // 2
    size = rows.shape[0] * rows.shape[1]
    return pl.pallas_call(
        read_kernel,
        out_shape=jax.ShapeDtypeStruct(rows.shape, jnp.bfloat16),
        in_specs=[VMEM] * 5 + [pl.BlockSpec(memory_space=pl.ANY)],
        out_specs=VMEM,
        compiler_params=params(16),
        cost_estimate=pl.CostEstimate(
            flops=4 * size * tokens * rows.shape[2], bytes_accessed=4 << 20, transcendentals=0
        ),
        name="read",
    )(rows, *document, after)


def fetch_kernel(first_row, w_hbm, w_ref, sem):
    copy = pltpu.make_async_copy(w_hbm.at[pl.ds(first_row, w_ref.shape[0]), :], w_ref, sem)
    copy.start()
    copy.wait()


def fetch(weight, first_row, row_count):
    return pl.pallas_call(
        functools.partial(fetch_kernel, first_row),
        out_shape=jax.ShapeDtypeStruct((row_count, weight.shape[1]), weight.dtype),
        in_specs=[HBM],
        out_specs=VMEM,
        scratch_shapes=[pltpu.SemaphoreType.DMA],
        compiler_params=params(2),
        cost_estimate=pl.CostEstimate(flops=0, bytes_accessed=4 << 20, transcendentals=0),
        name="fetch",
    )(in_hbm(weight))


def add_kernel(*refs):
    count = refs[0].shape[0]
    for slot in range(count):
        total = refs[0][slot].astype(jnp.float32)
        for ref in refs[1:-count]:
            total = total + ref[slot].astype(jnp.float32)
        refs[slot - count][...] = total.astype(refs[slot - count].dtype)


def add(parts):
    count = parts[0].shape[0]
    out = jax.ShapeDtypeStruct(parts[0].shape[1:], parts[0].dtype)
    return pl.pallas_call(
        add_kernel,
        out_shape=(out,) * count,
        in_specs=[VMEM] * len(parts),
        out_specs=(VMEM,) * count,
        compiler_params=params(4),
        name="add",
    )(*parts)


def project_kernel(part_count, *refs):
    part_refs, gain_ref, o_ref = refs[:part_count], refs[part_count], refs[-1]
    weight_refs = refs[part_count + 1 : -1]
    retained = part_refs[0][...].astype(jnp.float32)
    for part_ref in part_refs[1:]:
        retained = retained + part_ref[...].astype(jnp.float32)
    heads, _ = gain_ref.shape
    rows = retained.shape[0] // heads
    pieces = []
    for h in range(heads):
        one = retained[h * rows : (h + 1) * rows, :]
        mean_square = jnp.mean(one * one, axis=-1, keepdims=True)
        normed = one * lax.rsqrt(mean_square + 1e-06) * gain_ref[pl.ds(h, 1), :]
        pieces.append(normed.astype(jnp.bfloat16))
    flat = jnp.concatenate(pieces, axis=1)
    chunk = o_ref.shape[2]
    for g in range(o_ref.shape[0]):
        total, first = None, 0
        for weight_ref in weight_refs:
            last = first + weight_ref.shape[0]
            term = jnp.dot(
                flat[:, first:last],
                weight_ref[:, g * chunk : (g + 1) * chunk],
                preferred_element_type=jnp.float32,
            )
            total, first = term if total is None else total + term, last
        o_ref[g] = total.astype(o_ref.dtype)


def project(parts, gain, weights, groups):
    rows = parts[0].shape[0] // gain.shape[0]
    return pl.pallas_call(
        functools.partial(project_kernel, len(parts)),
        out_shape=jax.ShapeDtypeStruct((groups, rows, weights[0].shape[1] // groups), jnp.bfloat16),
        in_specs=[VMEM] * (len(parts) + 1 + len(weights)),
        out_specs=VMEM,
        compiler_params=params(24),
        name="project",
    )(*parts, gain, *weights)


def layer(queries, document_key_rows, document_value_rows, out_gain, out_weight):
    rows, heads, width = queries.shape
    tokens = document_key_rows.shape[0]
    head_groups = lax.axis_size("head")
    keys = document_key_rows.reshape(tokens, width)
    values = document_value_rows.reshape(tokens, width)
    own = jnp.transpose(queries, (1, 0, 2)).reshape(heads * rows, width)
    from_z = {}
    for steps in ORDER:
        from_z[steps] = exchange(own, steps, 0, steps >> 1)
    other_core = [(i, i ^ 1) for i in range(lax.axis_size("seq"))]
    near_keys = lax.ppermute(keys, "seq", other_core)
    near_values = lax.ppermute(values, "seq", other_core)
    staged_own, staged_keys, staged_values, gain, weight = stage(
        own,
        keys,
        values,
        out_gain,
        out_weight,
        row_counts=(heads * rows, tokens, tokens, heads, width),
    )
    column = join([staged_own, *(from_z[steps] for steps in range(1, Z_BLOCKS))])
    document = (staged_keys, staged_values, near_keys, near_values)
    from_x = {}
    for steps in ORDER:
        from_x[steps] = exchange(column, 0, steps, 1)
    part, parts = staged_own, []
    for steps in (0, *ORDER):
        part = read(from_x[steps] if steps else column, document, part)
        parts.append(exchange(part, 0, steps, 1) if steps else part)
    middle = width * (1 + (heads - 1) // 2)
    middle_weight = fetch(out_weight, width, middle - width)
    last_weight = fetch(out_weight, middle, heads * width - middle)
    weights = [weight, middle_weight, last_weight]
    slots = add(parts)
    parts = [slots[0]]
    for steps in ORDER:
        parts.append(exchange(slots[steps], steps, 0, steps >> 1))
    projected = project(parts, gain, weights, head_groups)
    pieces = lax.all_to_all(projected, "head", 0, 0, tiled=True)
    return jnp.sum(pieces.astype(jnp.float32), axis=0).astype(jnp.bfloat16)


def solution(mesh):
    in_specs = (
        P("seq", "head", None),
        P("seq", "head", None),
        P("seq", "head", None),
        P("head", None),
        P("head", None),
    )
    out_specs = P("seq", "head")
    return jax.shard_map(layer, mesh=mesh, in_specs=in_specs, out_specs=out_specs, check_vma=False)
```

```python
import functools

import jax
import jax.numpy as jnp
from jax import lax
from jax.experimental import pallas as pl
from jax.experimental.pallas import tpu as pltpu
from jax.sharding import PartitionSpec as P

CONTRACT_LAST = (((1,), (1,)), ((), ()))
KEY_TILE = 2048
TURN_TILE = 256
X_CHIPS, Z_BLOCKS, CORES = 4, 4, 2
ORDER = (2, 3, 1)
GROUPS = ((0,), (2,), (3, 1))


def seq_index(z_block, x_chip, core):
    return (z_block * X_CHIPS + x_chip) * CORES + core


def exchange(rows, z_step, x_step, core_step):
    pairs = []
    for z in range(Z_BLOCKS):
        for x in range(X_CHIPS):
            for core in range(CORES):
                to = seq_index(z ^ z_step, x ^ x_step, core ^ core_step)
                pairs.append((seq_index(z, x, core), to))
    return lax.ppermute(rows, "seq", pairs)


VMEM = pl.BlockSpec(memory_space=pltpu.VMEM)
HBM = pl.BlockSpec(memory_space=pltpu.HBM)


def in_hbm(array):
    return pltpu.with_memory_space_constraint(array, pltpu.HBM)


def params(mib):
    return pltpu.CompilerParams(vmem_limit_bytes=mib << 20)


def stage_kernel(
    q_hbm, k_hbm, v_hbm, g_hbm, w_hbm, q_ref, k_ref, vt_ref, g_ref, w_ref, v_ref, sems
):
    routes = (
        (v_hbm, v_ref),
        (k_hbm, k_ref),
        (q_hbm, q_ref),
        (g_hbm, g_ref),
        (w_hbm.at[pl.ds(0, w_ref.shape[0]), :], w_ref),
    )
    copies = [pltpu.make_async_copy(a, b, sems.at[i]) for i, (a, b) in enumerate(routes)]
    for copy in copies:
        copy.start()
    copies[0].wait()
    for start in range(0, v_ref.shape[0], TURN_TILE):
        vt_ref[:, start : start + TURN_TILE] = v_ref[pl.ds(start, TURN_TILE), :].T
    for copy in copies[1:]:
        copy.wait()


def stage(rows, keys, values, gain, weight, weight_rows):
    def like(array, *shape):
        return jax.ShapeDtypeStruct(shape or array.shape, array.dtype)

    return pl.pallas_call(
        stage_kernel,
        out_shape=(
            like(rows),
            like(keys),
            like(values, *values.shape[::-1]),
            like(gain),
            like(weight, weight_rows, weight.shape[1]),
        ),
        in_specs=[HBM] * 5,
        out_specs=(VMEM,) * 5,
        scratch_shapes=[
            pltpu.VMEM(values.shape, values.dtype),
            pltpu.SemaphoreType.DMA((5,)),
        ],
        compiler_params=params(6),
        cost_estimate=pl.CostEstimate(flops=0, bytes_accessed=4 << 20, transcendentals=0),
        name="stage",
    )(*(in_hbm(a) for a in (rows, keys, values, gain, weight)))


def join_kernel(*refs):
    for i, ref in enumerate(refs[:-1]):
        refs[-1][i] = ref[...]


def join(arrays):
    shape = (len(arrays),) + arrays[0].shape
    return pl.pallas_call(
        join_kernel,
        out_shape=jax.ShapeDtypeStruct(shape, arrays[0].dtype),
        in_specs=[VMEM] * len(arrays),
        out_specs=VMEM,
        compiler_params=params(2),
        name="join",
    )(*arrays)


def read_kernel(count, *refs):
    q_refs, document, o_refs = refs[:count], refs[count:-count], refs[-count:]
    slots, height, width = q_refs[0].shape
    rows = jnp.concatenate([r[...].reshape(slots * height, width) for r in q_refs], axis=0)
    total = None
    for k_ref, vt_ref in zip(document[::2], document[1::2]):
        for start in range(0, k_ref.shape[0], KEY_TILE):
            scores = lax.dot_general(
                k_ref[pl.ds(start, KEY_TILE), :],
                rows,
                CONTRACT_LAST,
                preferred_element_type=jnp.float32,
            )
            weights = (scores * scores).astype(jnp.bfloat16)
            term = jnp.dot(
                vt_ref[:, start : start + KEY_TILE], weights, preferred_element_type=jnp.float32
            )
            total = term if total is None else total + term
    result = total.T.astype(o_refs[0].dtype)
    for i, o_ref in enumerate(o_refs):
        first = i * slots * height
        o_ref[...] = result[first : first + slots * height, :].reshape(o_ref.shape)


def read(chunks, document):
    tokens = sum(a.shape[0] for a in document[::2])
    size = len(chunks) * chunks[0].size
    out = jax.ShapeDtypeStruct(chunks[0].shape, jnp.bfloat16)
    return pl.pallas_call(
        functools.partial(read_kernel, len(chunks)),
        out_shape=(out,) * len(chunks),
        in_specs=[VMEM] * (len(chunks) + len(document)),
        out_specs=(VMEM,) * len(chunks),
        compiler_params=params(32),
        cost_estimate=pl.CostEstimate(
            flops=4 * size * tokens, bytes_accessed=4 << 20, transcendentals=0
        ),
        name="read",
    )(*chunks, *document)


def fetch_kernel(first_row, w_hbm, w_ref, sem):
    copy = pltpu.make_async_copy(w_hbm.at[pl.ds(first_row, w_ref.shape[0]), :], w_ref, sem)
    copy.start()
    copy.wait()


def fetch(weight, first_row, row_count):
    return pl.pallas_call(
        functools.partial(fetch_kernel, first_row),
        out_shape=jax.ShapeDtypeStruct((row_count, weight.shape[1]), weight.dtype),
        in_specs=[HBM],
        out_specs=VMEM,
        scratch_shapes=[pltpu.SemaphoreType.DMA],
        compiler_params=params(2),
        cost_estimate=pl.CostEstimate(flops=0, bytes_accessed=4 << 20, transcendentals=0),
        name="fetch",
    )(in_hbm(weight))


def add_kernel(*refs):
    count = refs[0].shape[0]
    for slot in range(count):
        total = refs[0][slot].astype(jnp.float32)
        for ref in refs[1:-count]:
            total = total + ref[slot].astype(jnp.float32)
        refs[slot - count][...] = total.astype(refs[slot - count].dtype)


def add(parts):
    count = parts[0].shape[0]
    out = jax.ShapeDtypeStruct(parts[0].shape[1:], parts[0].dtype)
    return pl.pallas_call(
        add_kernel,
        out_shape=(out,) * count,
        in_specs=[VMEM] * len(parts),
        out_specs=(VMEM,) * count,
        compiler_params=params(4),
        name="add",
    )(*parts)


def project_kernel(part_count, *refs):
    part_refs, gain_ref, o_ref = refs[:part_count], refs[part_count], refs[-1]
    weight_refs = refs[part_count + 1 : -1]
    retained = part_refs[0][...].astype(jnp.float32)
    for part_ref in part_refs[1:]:
        retained = retained + part_ref[...].astype(jnp.float32)
    heads, _ = gain_ref.shape
    rows = retained.shape[0] // heads
    pieces = []
    for h in range(heads):
        one = retained[h * rows : (h + 1) * rows, :]
        mean_square = jnp.mean(one * one, axis=-1, keepdims=True)
        normed = one * lax.rsqrt(mean_square + 1e-06) * gain_ref[pl.ds(h, 1), :]
        pieces.append(normed.astype(jnp.bfloat16))
    flat = jnp.concatenate(pieces, axis=1)
    chunk = o_ref.shape[2]
    for g in range(o_ref.shape[0]):
        total, first = None, 0
        for weight_ref in weight_refs:
            last = first + weight_ref.shape[0]
            term = jnp.dot(
                flat[:, first:last],
                weight_ref[:, g * chunk : (g + 1) * chunk],
                preferred_element_type=jnp.float32,
            )
            total, first = term if total is None else total + term, last
        o_ref[g] = total.astype(o_ref.dtype)


def project(parts, gain, weights, groups):
    rows = parts[0].shape[0] // gain.shape[0]
    return pl.pallas_call(
        functools.partial(project_kernel, len(parts)),
        out_shape=jax.ShapeDtypeStruct((groups, rows, weights[0].shape[1] // groups), jnp.bfloat16),
        in_specs=[VMEM] * (len(parts) + 1 + len(weights)),
        out_specs=VMEM,
        compiler_params=params(24),
        name="project",
    )(*parts, gain, *weights)


def layer(queries, document_key_rows, document_value_rows, out_gain, out_weight):
    rows, heads, width = queries.shape
    tokens = document_key_rows.shape[0]
    head_groups = lax.axis_size("head")
    keys = document_key_rows.reshape(tokens, width)
    values = document_value_rows.reshape(tokens, width)
    own = jnp.transpose(queries, (1, 0, 2)).reshape(heads * rows, width)
    from_z = {}
    for steps in ORDER:
        from_z[steps] = exchange(own, steps, 0, steps >> 1)
    other_core = [(i, i ^ 1) for i in range(lax.axis_size("seq"))]
    near_keys = lax.ppermute(keys, "seq", other_core)
    staged_own, staged_keys, staged_turned, gain, weight = stage(
        own, keys, values, out_gain, out_weight, width
    )
    near_turned = lax.ppermute(staged_turned, "seq", other_core)
    column = join([staged_own, *(from_z[steps] for steps in range(1, Z_BLOCKS))])
    document = (staged_keys, staged_turned, near_keys, near_turned)
    from_x = {}
    for steps in ORDER:
        from_x[steps] = exchange(column, 0, steps, 1)
    parts = []
    for group in GROUPS:
        results = read(tuple(from_x[steps] if steps else column for steps in group), document)
        for steps, result in zip(group, results):
            parts.append(exchange(result, 0, steps, 1) if steps else result)
    middle = width * (1 + (heads - 1) // 2)
    middle_weight = fetch(out_weight, width, middle - width)
    last_weight = fetch(out_weight, middle, heads * width - middle)
    weights = [weight, middle_weight, last_weight]
    slots = add(parts)
    parts = [slots[0]]
    for steps in ORDER:
        parts.append(exchange(slots[steps], steps, 0, steps >> 1))
    projected = project(parts, gain, weights, head_groups)
    pieces = lax.all_to_all(projected, "head", 0, 0, tiled=True)
    return jnp.sum(pieces.astype(jnp.float32), axis=0).astype(jnp.bfloat16)


def solution(mesh):
    in_specs = (
        P("seq", "head", None),
        P("seq", "head", None),
        P("seq", "head", None),
        P("head", None),
        P("head", None),
    )
    out_specs = P("seq", "head")
    return jax.shard_map(layer, mesh=mesh, in_specs=in_specs, out_specs=out_specs, check_vma=False)
```

```python
import functools

import jax
import jax.numpy as jnp
from jax import lax
from jax.experimental import pallas as pl
from jax.experimental.pallas import tpu as pltpu
from jax.sharding import PartitionSpec as P

CONTRACT_LAST = (((1,), (1,)), ((), ()))
KEY_TILE = 2048
TURN_TILE = 256
X_CHIPS, Z_BLOCKS, CORES = 4, 4, 2
ORDER = (2, 3, 1)
GROUPS = ((0,), (2,), (3, 1))
Z_FLIPS = (0, 0, 1, 1)
X_FLIPS = (0, 1, 1, 0)


def seq_index(z_block, x_chip, core):
    return (z_block * X_CHIPS + x_chip) * CORES + core


def exchange(rows, z_step, x_step, core_step):
    pairs = []
    for z in range(Z_BLOCKS):
        for x in range(X_CHIPS):
            for core in range(CORES):
                to = seq_index(z ^ z_step, x ^ x_step, core ^ core_step)
                pairs.append((seq_index(z, x, core), to))
    return lax.ppermute(rows, "seq", pairs)


VMEM = pl.BlockSpec(memory_space=pltpu.VMEM)
HBM = pl.BlockSpec(memory_space=pltpu.HBM)


def in_hbm(array):
    return pltpu.with_memory_space_constraint(array, pltpu.HBM)


def params(mib):
    return pltpu.CompilerParams(vmem_limit_bytes=mib << 20)


def stage_kernel(
    q_hbm, k_hbm, v_hbm, g_hbm, w_hbm, q_ref, k_ref, vt_ref, g_ref, w_ref, v_ref, sems
):
    routes = (
        (v_hbm, v_ref),
        (k_hbm, k_ref),
        (q_hbm, q_ref),
        (g_hbm, g_ref),
        (w_hbm.at[pl.ds(0, w_ref.shape[0]), :], w_ref),
    )
    copies = [pltpu.make_async_copy(a, b, sems.at[i]) for i, (a, b) in enumerate(routes)]
    for copy in copies:
        copy.start()
    copies[0].wait()
    for start in range(0, v_ref.shape[0], TURN_TILE):
        vt_ref[:, start : start + TURN_TILE] = v_ref[pl.ds(start, TURN_TILE), :].T
    for copy in copies[1:]:
        copy.wait()


def stage(rows, keys, values, gain, weight, weight_rows):
    def like(array, *shape):
        return jax.ShapeDtypeStruct(shape or array.shape, array.dtype)

    return pl.pallas_call(
        stage_kernel,
        out_shape=(
            like(rows),
            like(keys),
            like(values, *values.shape[::-1]),
            like(gain),
            like(weight, weight_rows, weight.shape[1]),
        ),
        in_specs=[HBM] * 5,
        out_specs=(VMEM,) * 5,
        scratch_shapes=[
            pltpu.VMEM(values.shape, values.dtype),
            pltpu.SemaphoreType.DMA((5,)),
        ],
        compiler_params=params(6),
        cost_estimate=pl.CostEstimate(flops=0, bytes_accessed=4 << 20, transcendentals=0),
        name="stage",
    )(*(in_hbm(a) for a in (rows, keys, values, gain, weight)))


def join_kernel(*refs):
    for i, ref in enumerate(refs[:-1]):
        refs[-1][i] = ref[...]


def join(arrays):
    shape = (len(arrays),) + arrays[0].shape
    return pl.pallas_call(
        join_kernel,
        out_shape=jax.ShapeDtypeStruct(shape, arrays[0].dtype),
        in_specs=[VMEM] * len(arrays),
        out_specs=VMEM,
        compiler_params=params(2),
        name="join",
    )(*arrays)


def read_kernel(count, *refs):
    q_refs, document, o_refs = refs[:count], refs[count:-count], refs[-count:]
    slots, height, width = q_refs[0].shape
    rows = jnp.concatenate([r[...].reshape(slots * height, width) for r in q_refs], axis=0)
    total = None
    for k_ref, vt_ref in zip(document[::2], document[1::2]):
        for start in range(0, k_ref.shape[0], KEY_TILE):
            scores = lax.dot_general(
                k_ref[pl.ds(start, KEY_TILE), :],
                rows,
                CONTRACT_LAST,
                preferred_element_type=jnp.float32,
            )
            weights = (scores * scores).astype(jnp.bfloat16)
            term = jnp.dot(
                vt_ref[:, start : start + KEY_TILE], weights, preferred_element_type=jnp.float32
            )
            total = term if total is None else total + term
    result = total.T.astype(o_refs[0].dtype)
    for i, o_ref in enumerate(o_refs):
        first = i * slots * height
        o_ref[...] = result[first : first + slots * height, :].reshape(o_ref.shape)


def read(chunks, document):
    tokens = sum(a.shape[0] for a in document[::2])
    size = len(chunks) * chunks[0].size
    out = jax.ShapeDtypeStruct(chunks[0].shape, jnp.bfloat16)
    return pl.pallas_call(
        functools.partial(read_kernel, len(chunks)),
        out_shape=(out,) * len(chunks),
        in_specs=[VMEM] * (len(chunks) + len(document)),
        out_specs=(VMEM,) * len(chunks),
        compiler_params=params(32),
        cost_estimate=pl.CostEstimate(
            flops=4 * size * tokens, bytes_accessed=4 << 20, transcendentals=0
        ),
        name="read",
    )(*chunks, *document)


def fetch_kernel(first_row, w_hbm, w_ref, sem):
    copy = pltpu.make_async_copy(w_hbm.at[pl.ds(first_row, w_ref.shape[0]), :], w_ref, sem)
    copy.start()
    copy.wait()


def fetch(weight, first_row, row_count):
    return pl.pallas_call(
        functools.partial(fetch_kernel, first_row),
        out_shape=jax.ShapeDtypeStruct((row_count, weight.shape[1]), weight.dtype),
        in_specs=[HBM],
        out_specs=VMEM,
        scratch_shapes=[pltpu.SemaphoreType.DMA],
        compiler_params=params(2),
        cost_estimate=pl.CostEstimate(flops=0, bytes_accessed=4 << 20, transcendentals=0),
        name="fetch",
    )(in_hbm(weight))


def add_kernel(*refs):
    count = refs[0].shape[0]
    for slot in range(count):
        total = refs[0][slot].astype(jnp.float32)
        for ref in refs[1:-count]:
            total = total + ref[slot].astype(jnp.float32)
        refs[slot - count][...] = total.astype(refs[slot - count].dtype)


def add(parts):
    count = parts[0].shape[0]
    out = jax.ShapeDtypeStruct(parts[0].shape[1:], parts[0].dtype)
    return pl.pallas_call(
        add_kernel,
        out_shape=(out,) * count,
        in_specs=[VMEM] * len(parts),
        out_specs=(VMEM,) * count,
        compiler_params=params(4),
        name="add",
    )(*parts)


def project_kernel(part_count, *refs):
    part_refs, gain_ref, o_ref = refs[:part_count], refs[part_count], refs[-1]
    weight_refs = refs[part_count + 1 : -1]
    retained = part_refs[0][...].astype(jnp.float32)
    for part_ref in part_refs[1:]:
        retained = retained + part_ref[...].astype(jnp.float32)
    heads, _ = gain_ref.shape
    rows = retained.shape[0] // heads
    pieces = []
    for h in range(heads):
        one = retained[h * rows : (h + 1) * rows, :]
        mean_square = jnp.mean(one * one, axis=-1, keepdims=True)
        normed = one * lax.rsqrt(mean_square + 1e-06) * gain_ref[pl.ds(h, 1), :]
        pieces.append(normed.astype(jnp.bfloat16))
    flat = jnp.concatenate(pieces, axis=1)
    chunk = o_ref.shape[2]
    for g in range(o_ref.shape[0]):
        total, first = None, 0
        for weight_ref in weight_refs:
            last = first + weight_ref.shape[0]
            term = jnp.dot(
                flat[:, first:last],
                weight_ref[:, g * chunk : (g + 1) * chunk],
                preferred_element_type=jnp.float32,
            )
            total, first = term if total is None else total + term, last
        o_ref[g] = total.astype(o_ref.dtype)


def project(parts, gain, weights, groups):
    rows = parts[0].shape[0] // gain.shape[0]
    return pl.pallas_call(
        functools.partial(project_kernel, len(parts)),
        out_shape=jax.ShapeDtypeStruct((groups, rows, weights[0].shape[1] // groups), jnp.bfloat16),
        in_specs=[VMEM] * (len(parts) + 1 + len(weights)),
        out_specs=VMEM,
        compiler_params=params(24),
        name="project",
    )(*parts, gain, *weights)


def layer(queries, document_key_rows, document_value_rows, out_gain, out_weight):
    rows, heads, width = queries.shape
    tokens = document_key_rows.shape[0]
    head_groups = lax.axis_size("head")
    keys = document_key_rows.reshape(tokens, width)
    values = document_value_rows.reshape(tokens, width)
    own = jnp.transpose(queries, (1, 0, 2)).reshape(heads * rows, width)
    from_z = {}
    for steps in ORDER:
        from_z[steps] = exchange(own, steps, 0, Z_FLIPS[steps])
    other_core = [(i, i ^ 1) for i in range(lax.axis_size("seq"))]
    near_keys = lax.ppermute(keys, "seq", other_core)
    staged_own, staged_keys, staged_turned, gain, weight = stage(
        own, keys, values, out_gain, out_weight, width
    )
    near_turned = lax.ppermute(staged_turned, "seq", other_core)
    column = join([staged_own, *(from_z[steps] for steps in range(1, Z_BLOCKS))])
    document = (staged_keys, staged_turned, near_keys, near_turned)
    from_x = {}
    for steps in ORDER:
        from_x[steps] = exchange(column, 0, steps, X_FLIPS[steps])
    parts = []
    for group in GROUPS:
        results = read(tuple(from_x[steps] if steps else column for steps in group), document)
        for steps, result in zip(group, results):
            parts.append(exchange(result, 0, steps, X_FLIPS[steps]) if steps else result)
    middle = width * (1 + (heads - 1) // 2)
    middle_weight = fetch(out_weight, width, middle - width)
    last_weight = fetch(out_weight, middle, heads * width - middle)
    weights = [weight, middle_weight, last_weight]
    slots = add(parts)
    parts = [slots[0]]
    for steps in ORDER:
        parts.append(exchange(slots[steps], steps, 0, Z_FLIPS[steps]))
    projected = project(parts, gain, weights, head_groups)
    pieces = lax.all_to_all(projected, "head", 0, 0, tiled=True)
    return jnp.sum(pieces.astype(jnp.float32), axis=0).astype(jnp.bfloat16)


def solution(mesh):
    in_specs = (
        P("seq", "head", None),
        P("seq", "head", None),
        P("seq", "head", None),
        P("head", None),
        P("head", None),
    )
    out_specs = P("seq", "head")
    return jax.shard_map(layer, mesh=mesh, in_specs=in_specs, out_specs=out_specs, check_vma=False)
```

```python
import functools

import jax
import jax.numpy as jnp
from jax import lax
from jax.experimental import pallas as pl
from jax.experimental.pallas import tpu as pltpu
from jax.sharding import PartitionSpec as P

CONTRACT_LAST = (((1,), (1,)), ((), ()))
KEY_TILE = 2048
TURN_TILE = 256
X_CHIPS, Z_BLOCKS, CORES = 4, 4, 2
ORDER = (2, 3, 1)
GROUPS = ((0,), (2,), (3, 1))
Z_FLIPS = (0, 0, 1, 0)
X_FLIPS = (0, 1, 1, 0)


def seq_index(z_block, x_chip, core):
    return (z_block * X_CHIPS + x_chip) * CORES + core


def exchange(rows, z_step, x_step, core_step):
    pairs = []
    for z in range(Z_BLOCKS):
        for x in range(X_CHIPS):
            for core in range(CORES):
                to = seq_index(z ^ z_step, x ^ x_step, core ^ core_step)
                pairs.append((seq_index(z, x, core), to))
    return lax.ppermute(rows, "seq", pairs)


VMEM = pl.BlockSpec(memory_space=pltpu.VMEM)
HBM = pl.BlockSpec(memory_space=pltpu.HBM)


def in_hbm(array):
    return pltpu.with_memory_space_constraint(array, pltpu.HBM)


def params(mib):
    return pltpu.CompilerParams(vmem_limit_bytes=mib << 20)


def stage_kernel(
    q_hbm, k_hbm, v_hbm, g_hbm, w_hbm, q_ref, k_ref, vt_ref, g_ref, w_ref, v_ref, sems
):
    routes = (
        (v_hbm, v_ref),
        (k_hbm, k_ref),
        (q_hbm, q_ref),
        (g_hbm, g_ref),
        (w_hbm.at[pl.ds(0, w_ref.shape[0]), :], w_ref),
    )
    copies = [pltpu.make_async_copy(a, b, sems.at[i]) for i, (a, b) in enumerate(routes)]
    for copy in copies:
        copy.start()
    copies[0].wait()
    for start in range(0, v_ref.shape[0], TURN_TILE):
        vt_ref[:, start : start + TURN_TILE] = v_ref[pl.ds(start, TURN_TILE), :].T
    for copy in copies[1:]:
        copy.wait()


def stage(rows, keys, values, gain, weight, weight_rows):
    def like(array, *shape):
        return jax.ShapeDtypeStruct(shape or array.shape, array.dtype)

    return pl.pallas_call(
        stage_kernel,
        out_shape=(
            like(rows),
            like(keys),
            like(values, *values.shape[::-1]),
            like(gain),
            like(weight, weight_rows, weight.shape[1]),
        ),
        in_specs=[HBM] * 5,
        out_specs=(VMEM,) * 5,
        scratch_shapes=[
            pltpu.VMEM(values.shape, values.dtype),
            pltpu.SemaphoreType.DMA((5,)),
        ],
        compiler_params=params(6),
        cost_estimate=pl.CostEstimate(flops=0, bytes_accessed=4 << 20, transcendentals=0),
        name="stage",
    )(*(in_hbm(a) for a in (rows, keys, values, gain, weight)))


def join_kernel(*refs):
    for i, ref in enumerate(refs[:-1]):
        refs[-1][i] = ref[...]


def join(arrays):
    shape = (len(arrays),) + arrays[0].shape
    return pl.pallas_call(
        join_kernel,
        out_shape=jax.ShapeDtypeStruct(shape, arrays[0].dtype),
        in_specs=[VMEM] * len(arrays),
        out_specs=VMEM,
        compiler_params=params(2),
        name="join",
    )(*arrays)


def read_kernel(count, *refs):
    q_refs, document, o_refs = refs[:count], refs[count:-count], refs[-count:]
    slots, height, width = q_refs[0].shape
    rows = jnp.concatenate([r[...].reshape(slots * height, width) for r in q_refs], axis=0)
    total = None
    for k_ref, vt_ref in zip(document[::2], document[1::2]):
        for start in range(0, k_ref.shape[0], KEY_TILE):
            scores = lax.dot_general(
                k_ref[pl.ds(start, KEY_TILE), :],
                rows,
                CONTRACT_LAST,
                preferred_element_type=jnp.float32,
            )
            weights = (scores * scores).astype(jnp.bfloat16)
            term = jnp.dot(
                vt_ref[:, start : start + KEY_TILE], weights, preferred_element_type=jnp.float32
            )
            total = term if total is None else total + term
    result = total.T.astype(o_refs[0].dtype)
    for i, o_ref in enumerate(o_refs):
        first = i * slots * height
        o_ref[...] = result[first : first + slots * height, :].reshape(o_ref.shape)


def read(chunks, document):
    tokens = sum(a.shape[0] for a in document[::2])
    size = len(chunks) * chunks[0].size
    out = jax.ShapeDtypeStruct(chunks[0].shape, jnp.bfloat16)
    return pl.pallas_call(
        functools.partial(read_kernel, len(chunks)),
        out_shape=(out,) * len(chunks),
        in_specs=[VMEM] * (len(chunks) + len(document)),
        out_specs=(VMEM,) * len(chunks),
        compiler_params=params(32),
        cost_estimate=pl.CostEstimate(
            flops=4 * size * tokens, bytes_accessed=4 << 20, transcendentals=0
        ),
        name="read",
    )(*chunks, *document)


def fetch_kernel(first_row, w_hbm, w_ref, sem):
    copy = pltpu.make_async_copy(w_hbm.at[pl.ds(first_row, w_ref.shape[0]), :], w_ref, sem)
    copy.start()
    copy.wait()


def fetch(weight, first_row, row_count):
    return pl.pallas_call(
        functools.partial(fetch_kernel, first_row),
        out_shape=jax.ShapeDtypeStruct((row_count, weight.shape[1]), weight.dtype),
        in_specs=[HBM],
        out_specs=VMEM,
        scratch_shapes=[pltpu.SemaphoreType.DMA],
        compiler_params=params(2),
        cost_estimate=pl.CostEstimate(flops=0, bytes_accessed=4 << 20, transcendentals=0),
        name="fetch",
    )(in_hbm(weight))


def add_kernel(*refs):
    count = refs[0].shape[0]
    for slot in range(count):
        total = refs[0][slot].astype(jnp.float32)
        for ref in refs[1:-count]:
            total = total + ref[slot].astype(jnp.float32)
        refs[slot - count][...] = total.astype(refs[slot - count].dtype)


def add(parts):
    count = parts[0].shape[0]
    out = jax.ShapeDtypeStruct(parts[0].shape[1:], parts[0].dtype)
    return pl.pallas_call(
        add_kernel,
        out_shape=(out,) * count,
        in_specs=[VMEM] * len(parts),
        out_specs=(VMEM,) * count,
        compiler_params=params(4),
        name="add",
    )(*parts)


def project_kernel(part_count, *refs):
    part_refs, gain_ref, o_ref = refs[:part_count], refs[part_count], refs[-1]
    weight_refs = refs[part_count + 1 : -1]
    retained = part_refs[0][...].astype(jnp.float32)
    for part_ref in part_refs[1:]:
        retained = retained + part_ref[...].astype(jnp.float32)
    heads, _ = gain_ref.shape
    rows = retained.shape[0] // heads
    pieces = []
    for h in range(heads):
        one = retained[h * rows : (h + 1) * rows, :]
        mean_square = jnp.mean(one * one, axis=-1, keepdims=True)
        normed = one * lax.rsqrt(mean_square + 1e-06) * gain_ref[pl.ds(h, 1), :]
        pieces.append(normed.astype(jnp.bfloat16))
    flat = jnp.concatenate(pieces, axis=1)
    chunk = o_ref.shape[2]
    for g in range(o_ref.shape[0]):
        total, first = None, 0
        for weight_ref in weight_refs:
            last = first + weight_ref.shape[0]
            term = jnp.dot(
                flat[:, first:last],
                weight_ref[:, g * chunk : (g + 1) * chunk],
                preferred_element_type=jnp.float32,
            )
            total, first = term if total is None else total + term, last
        o_ref[g] = total.astype(o_ref.dtype)


def project(parts, gain, weights, groups):
    rows = parts[0].shape[0] // gain.shape[0]
    return pl.pallas_call(
        functools.partial(project_kernel, len(parts)),
        out_shape=jax.ShapeDtypeStruct((groups, rows, weights[0].shape[1] // groups), jnp.bfloat16),
        in_specs=[VMEM] * (len(parts) + 1 + len(weights)),
        out_specs=VMEM,
        compiler_params=params(24),
        name="project",
    )(*parts, gain, *weights)


def sum_kernel(p_ref, o_ref):
    o_ref[...] = jnp.sum(p_ref[...].astype(jnp.float32), axis=0).astype(o_ref.dtype)


def sum_pieces(pieces):
    return pl.pallas_call(
        sum_kernel,
        out_shape=jax.ShapeDtypeStruct(pieces.shape[1:], pieces.dtype),
        in_specs=[VMEM],
        out_specs=VMEM,
        compiler_params=params(2),
        name="sum_pieces",
    )(pieces)


def layer(queries, document_key_rows, document_value_rows, out_gain, out_weight):
    rows, heads, width = queries.shape
    tokens = document_key_rows.shape[0]
    head_groups = lax.axis_size("head")
    keys = document_key_rows.reshape(tokens, width)
    values = document_value_rows.reshape(tokens, width)
    own = jnp.transpose(queries, (1, 0, 2)).reshape(heads * rows, width)
    from_z = {}
    for steps in ORDER:
        from_z[steps] = exchange(own, steps, 0, Z_FLIPS[steps])
    other_core = [(i, i ^ 1) for i in range(lax.axis_size("seq"))]
    near_keys = lax.ppermute(keys, "seq", other_core)
    staged_own, staged_keys, staged_turned, gain, weight = stage(
        own, keys, values, out_gain, out_weight, width
    )
    near_turned = lax.ppermute(staged_turned, "seq", other_core)
    column = join([staged_own, *(from_z[steps] for steps in range(1, Z_BLOCKS))])
    document = (staged_keys, staged_turned, near_keys, near_turned)
    from_x = {}
    for steps in ORDER:
        from_x[steps] = exchange(column, 0, steps, X_FLIPS[steps])
    parts = []
    for group in GROUPS:
        results = read(tuple(from_x[steps] if steps else column for steps in group), document)
        for steps, result in zip(group, results):
            parts.append(exchange(result, 0, steps, X_FLIPS[steps]) if steps else result)
    middle = width * (1 + (heads - 1) // 2)
    middle_weight = fetch(out_weight, width, middle - width)
    last_weight = fetch(out_weight, middle, heads * width - middle)
    weights = [weight, middle_weight, last_weight]
    slots = add(parts)
    parts = [slots[0]]
    for steps in ORDER:
        parts.append(exchange(slots[steps], steps, 0, Z_FLIPS[steps]))
    projected = project(parts, gain, weights, head_groups)
    pieces = lax.all_to_all(projected, "head", 0, 0, tiled=True)
    return sum_pieces(pieces)


def solution(mesh):
    in_specs = (
        P("seq", "head", None),
        P("seq", "head", None),
        P("seq", "head", None),
        P("head", None),
        P("head", None),
    )
    out_specs = P("seq", "head")
    return jax.shard_map(layer, mesh=mesh, in_specs=in_specs, out_specs=out_specs, check_vma=False)
```

```python
import functools

import jax
import jax.numpy as jnp
from jax import lax
from jax.experimental import pallas as pl
from jax.experimental.pallas import tpu as pltpu
from jax.sharding import PartitionSpec as P

CONTRACT_LAST = (((1,), (1,)), ((), ()))
KEY_TILE = 2048
TURN_TILE = 256
X_CHIPS, Z_BLOCKS, CORES = 4, 4, 2
ORDER = (2, 3, 1)
GROUPS = ((0,), (2,), (3, 1))
Z_FLIPS = (0, 0, 1, 1)
X_FLIPS = (0, 1, 1, 0)


def seq_index(z_block, x_chip, core):
    return (z_block * X_CHIPS + x_chip) * CORES + core


def exchange(rows, z_step, x_step, core_step):
    pairs = []
    for z in range(Z_BLOCKS):
        for x in range(X_CHIPS):
            for core in range(CORES):
                to = seq_index(z ^ z_step, x ^ x_step, core ^ core_step)
                pairs.append((seq_index(z, x, core), to))
    return lax.ppermute(rows, "seq", pairs)


VMEM = pl.BlockSpec(memory_space=pltpu.VMEM)
HBM = pl.BlockSpec(memory_space=pltpu.HBM)


def in_hbm(array):
    return pltpu.with_memory_space_constraint(array, pltpu.HBM)


def params(mib):
    return pltpu.CompilerParams(vmem_limit_bytes=mib << 20)


def stage_kernel(
    q_hbm, k_hbm, v_hbm, g_hbm, q_ref, k_ref, vt_ref, g_ref, v_ref, sems
):
    routes = (
        (v_hbm, v_ref),
        (k_hbm, k_ref),
        (q_hbm, q_ref),
        (g_hbm, g_ref),
    )
    copies = [pltpu.make_async_copy(a, b, sems.at[i]) for i, (a, b) in enumerate(routes)]
    for copy in copies:
        copy.start()
    copies[0].wait()
    for start in range(0, v_ref.shape[0], TURN_TILE):
        vt_ref[:, start : start + TURN_TILE] = v_ref[pl.ds(start, TURN_TILE), :].T
    for copy in copies[1:]:
        copy.wait()


def stage(rows, keys, values, gain):
    def like(array, *shape):
        return jax.ShapeDtypeStruct(shape or array.shape, array.dtype)

    return pl.pallas_call(
        stage_kernel,
        out_shape=(
            like(rows),
            like(keys),
            like(values, *values.shape[::-1]),
            like(gain),
        ),
        in_specs=[HBM] * 4,
        out_specs=(VMEM,) * 4,
        scratch_shapes=[
            pltpu.VMEM(values.shape, values.dtype),
            pltpu.SemaphoreType.DMA((4,)),
        ],
        compiler_params=params(6),
        cost_estimate=pl.CostEstimate(flops=0, bytes_accessed=4 << 20, transcendentals=0),
        name="stage",
    )(*(in_hbm(a) for a in (rows, keys, values, gain)))


def join_kernel(*refs):
    for i, ref in enumerate(refs[:-1]):
        refs[-1][i] = ref[...]


def join(arrays):
    shape = (len(arrays),) + arrays[0].shape
    return pl.pallas_call(
        join_kernel,
        out_shape=jax.ShapeDtypeStruct(shape, arrays[0].dtype),
        in_specs=[VMEM] * len(arrays),
        out_specs=VMEM,
        compiler_params=params(2),
        name="join",
    )(*arrays)


def read_kernel(count, *refs):
    q_refs, document, o_refs = refs[:count], refs[count:-count], refs[-count:]
    slots, height, width = q_refs[0].shape
    rows = jnp.concatenate([r[...].reshape(slots * height, width) for r in q_refs], axis=0)
    total = None
    for k_ref, vt_ref in zip(document[::2], document[1::2]):
        for start in range(0, k_ref.shape[0], KEY_TILE):
            scores = lax.dot_general(
                k_ref[pl.ds(start, KEY_TILE), :],
                rows,
                CONTRACT_LAST,
                preferred_element_type=jnp.float32,
            )
            weights = (scores * scores).astype(jnp.bfloat16)
            term = jnp.dot(
                vt_ref[:, start : start + KEY_TILE], weights, preferred_element_type=jnp.float32
            )
            total = term if total is None else total + term
    result = total.T.astype(o_refs[0].dtype)
    for i, o_ref in enumerate(o_refs):
        first = i * slots * height
        o_ref[...] = result[first : first + slots * height, :].reshape(o_ref.shape)


def read(chunks, document):
    tokens = sum(a.shape[0] for a in document[::2])
    size = len(chunks) * chunks[0].size
    out = jax.ShapeDtypeStruct(chunks[0].shape, jnp.bfloat16)
    return pl.pallas_call(
        functools.partial(read_kernel, len(chunks)),
        out_shape=(out,) * len(chunks),
        in_specs=[VMEM] * (len(chunks) + len(document)),
        out_specs=(VMEM,) * len(chunks),
        compiler_params=params(32),
        cost_estimate=pl.CostEstimate(
            flops=4 * size * tokens, bytes_accessed=4 << 20, transcendentals=0
        ),
        name="read",
    )(*chunks, *document)


def fetch_kernel(first_row, w_hbm, w_ref, sem):
    copy = pltpu.make_async_copy(w_hbm.at[pl.ds(first_row, w_ref.shape[0]), :], w_ref, sem)
    copy.start()
    copy.wait()


def fetch(weight, first_row, row_count):
    return pl.pallas_call(
        functools.partial(fetch_kernel, first_row),
        out_shape=jax.ShapeDtypeStruct((row_count, weight.shape[1]), weight.dtype),
        in_specs=[HBM],
        out_specs=VMEM,
        scratch_shapes=[pltpu.SemaphoreType.DMA],
        compiler_params=params(2),
        cost_estimate=pl.CostEstimate(flops=0, bytes_accessed=4 << 20, transcendentals=0),
        name="fetch",
    )(in_hbm(weight))


def add_kernel(*refs):
    count = refs[0].shape[0]
    for slot in range(count):
        total = refs[0][slot].astype(jnp.float32)
        for ref in refs[1:-count]:
            total = total + ref[slot].astype(jnp.float32)
        refs[slot - count][...] = total.astype(refs[slot - count].dtype)


def add(parts):
    count = parts[0].shape[0]
    out = jax.ShapeDtypeStruct(parts[0].shape[1:], parts[0].dtype)
    return pl.pallas_call(
        add_kernel,
        out_shape=(out,) * count,
        in_specs=[VMEM] * len(parts),
        out_specs=(VMEM,) * count,
        compiler_params=params(4),
        name="add",
    )(*parts)


def project_kernel(part_count, *refs):
    part_refs, gain_ref, o_ref = refs[:part_count], refs[part_count], refs[-1]
    weight_refs = refs[part_count + 1 : -1]
    retained = part_refs[0][...].astype(jnp.float32)
    for part_ref in part_refs[1:]:
        retained = retained + part_ref[...].astype(jnp.float32)
    heads, _ = gain_ref.shape
    rows = retained.shape[0] // heads
    pieces = []
    for h in range(heads):
        one = retained[h * rows : (h + 1) * rows, :]
        mean_square = jnp.mean(one * one, axis=-1, keepdims=True)
        normed = one * lax.rsqrt(mean_square + 1e-06) * gain_ref[pl.ds(h, 1), :]
        pieces.append(normed.astype(jnp.bfloat16))
    flat = jnp.concatenate(pieces, axis=1)
    chunk = o_ref.shape[2]
    for g in range(o_ref.shape[0]):
        total, first = None, 0
        for weight_ref in weight_refs:
            last = first + weight_ref.shape[0]
            term = jnp.dot(
                flat[:, first:last],
                weight_ref[:, g * chunk : (g + 1) * chunk],
                preferred_element_type=jnp.float32,
            )
            total, first = term if total is None else total + term, last
        o_ref[g] = total.astype(o_ref.dtype)


def project(parts, gain, weights, groups):
    rows = parts[0].shape[0] // gain.shape[0]
    return pl.pallas_call(
        functools.partial(project_kernel, len(parts)),
        out_shape=jax.ShapeDtypeStruct((groups, rows, weights[0].shape[1] // groups), jnp.bfloat16),
        in_specs=[VMEM] * (len(parts) + 1 + len(weights)),
        out_specs=VMEM,
        compiler_params=params(24),
        name="project",
    )(*parts, gain, *weights)


def layer(queries, document_key_rows, document_value_rows, out_gain, out_weight):
    rows, heads, width = queries.shape
    tokens = document_key_rows.shape[0]
    head_groups = lax.axis_size("head")
    keys = document_key_rows.reshape(tokens, width)
    values = document_value_rows.reshape(tokens, width)
    own = jnp.transpose(queries, (1, 0, 2)).reshape(heads * rows, width)
    from_z = {}
    for steps in ORDER:
        from_z[steps] = exchange(own, steps, 0, Z_FLIPS[steps])
    other_core = [(i, i ^ 1) for i in range(lax.axis_size("seq"))]
    near_keys = lax.ppermute(keys, "seq", other_core)
    staged_own, staged_keys, staged_turned, gain = stage(own, keys, values, out_gain)
    near_turned = lax.ppermute(staged_turned, "seq", other_core)
    column = join([staged_own, *(from_z[steps] for steps in range(1, Z_BLOCKS))])
    document = (staged_keys, staged_turned, near_keys, near_turned)
    from_x = {}
    for steps in ORDER:
        from_x[steps] = exchange(column, 0, steps, X_FLIPS[steps])
    parts = []
    for group in GROUPS:
        results = read(tuple(from_x[steps] if steps else column for steps in group), document)
        for steps, result in zip(group, results):
            parts.append(exchange(result, 0, steps, X_FLIPS[steps]) if steps else result)
    middle = width * (heads // 2)
    middle_weight = fetch(out_weight, 0, middle)
    last_weight = fetch(out_weight, middle, heads * width - middle)
    weights = [middle_weight, last_weight]
    slots = add(parts)
    parts = [slots[0]]
    for steps in ORDER:
        parts.append(exchange(slots[steps], steps, 0, Z_FLIPS[steps]))
    projected = project(parts, gain, weights, head_groups)
    pieces = lax.all_to_all(projected, "head", 0, 0, tiled=True)
    return jnp.sum(pieces.astype(jnp.float32), axis=0).astype(jnp.bfloat16)


def solution(mesh):
    in_specs = (
        P("seq", "head", None),
        P("seq", "head", None),
        P("seq", "head", None),
        P("head", None),
        P("head", None),
    )
    out_specs = P("seq", "head")
    return jax.shard_map(layer, mesh=mesh, in_specs=in_specs, out_specs=out_specs, check_vma=False)
```
